512 devices in a mesh: row: 32 (over z, x), col: 16 (over y, core).
Axes of the slice: x: 4, y: 8, z: 8, core: 2. Of those that a mesh axis runs over, the one named last changes fastest.
Arguments:
- source_points: float32 [3, 65536], P(None, 'row'), may hold values from -4 to 4
- target_points: float32 [3, 262144], P(None, 'col'), may hold values from -4 to 4
- source_potential: float32 [65536], P('row'), may hold values from -2.5 to 3.6
- target_potential: float32 [262144], P('col'), may hold values from -2.5 to 3.6
- neighbours: int32 [256, 64], P('row'), may hold values from -1 to 1023, as said below
Outputs:
- source_dual: float32 [65536], P('row')
- target_dual: float32 [262144], P('col')
The draws below stay inside these ranges and needn't reach their ends.
Inputs may be any that keep to these rules, and one draw needn't show every extreme that they name: `neighbours`: each row block lists, in increasing order, between 32 and 64 distinct column-block ids, then -1 up to 64 entries; some row block lists 64; every column block is listed by at least one row block.
All inputs are finite; a program needn't handle non-finite values.
Results may differ from the reference program's by a relative error of at most 0.0003.
Values sent between devices are 32-bit elements; how exact they have to be, the bound alone decides.
No kernel may reach another device: no remote copies, remote signals or barrier semaphores. Data moves between devices by JAX's collectives and lax.ppermute only.
A program may use at most 64 MiB of HBM per device.

```python
import jax
import jax.numpy as jnp
from jax import lax

BLOCK = 256
NBR_MOST = 64
ITERS = 2
CB_DEV = 64
ROW_BLOCKS = 256
COL_BLOCKS = 1024
SOURCES = 65536
TARGETS = 262144
N_COL = 16


def potential_values(key, amount):
    values = 0.5 * jax.random.normal(key, (amount,), jnp.float32)
    return jnp.clip(values, -2.5, 2.5).astype(jnp.float32)


def draw_source_potential(key, part):
    return potential_values(jax.random.fold_in(key, 11), SOURCES)


def draw_target_potential(key, part):
    return potential_values(jax.random.fold_in(key, 23), TARGETS)


def draw_neighbours(key, part):
    first, second, third, fourth = jax.random.split(jax.random.fold_in(key, 37), 4)
    columns = jnp.arange(COL_BLOCKS, dtype=jnp.int32)
    row_ids = jnp.arange(ROW_BLOCKS, dtype=jnp.int32)
    owner_weight = jax.random.randint(first, (N_COL,), 0, 4, dtype=jnp.int32) * 8192
    noise = jax.random.randint(second, (ROW_BLOCKS, COL_BLOCKS), 0, 16384, dtype=jnp.int32)
    scores = noise + owner_weight[columns // CB_DEV][None, :]
    period = min(ROW_BLOCKS, COL_BLOCKS)
    forced = columns[None, :] % period == row_ids[:, None] % period
    scores = jnp.where(forced, scores + 65536, scores)
    scores = scores * COL_BLOCKS + columns[None, :]
    unused, picked = lax.top_k(scores, NBR_MOST)
    lengths = jax.random.randint(third, (ROW_BLOCKS,), NBR_MOST // 2, NBR_MOST + 1, dtype=jnp.int32)
    full_row = jax.random.randint(fourth, (), 0, ROW_BLOCKS, dtype=jnp.int32)
    lengths = jnp.where(row_ids == full_row, NBR_MOST, lengths)
    keep = jnp.arange(NBR_MOST, dtype=jnp.int32)[None, :] < lengths[:, None]
    listed = jnp.where(keep, picked.astype(jnp.int32), COL_BLOCKS)
    listed = jnp.sort(listed, axis=1)
    return jnp.where(listed == COL_BLOCKS, -1, listed).astype(jnp.int32)


def block_scale(rng, extent, pieces, least, largest):
    def one(axis_at, blocks):
        steps = jax.random.uniform(jax.random.fold_in(jax.random.fold_in(rng, 6), axis_at), (blocks,), jnp.float32, least / len(pieces), largest / len(pieces))
        return jnp.repeat(jnp.exp(steps), extent[axis_at] // blocks).reshape((-1,) + (1,) * (len(extent) - axis_at - 1))

    gain = one(*pieces[0])
    for cut in pieces[1:]:
        gain = gain * one(*cut)
    return gain


def bell_draw(own_key, shape, scale, most, pieces=(), kind=jnp.bfloat16):
    array = jax.random.normal(own_key, shape, jnp.float32) * scale
    if len(pieces) > 0:
        array = block_scale(own_key, shape, pieces, -0.22, 0.18) * array
    return jnp.clip(array, min=-most, max=most).astype(kind)


def setup_inputs(seed: int = 0) -> dict:
    splits = jax.random.split(jax.random.key(seed), 6)
    source_points = bell_draw(splits[0], (3, SOURCES), 1.0, 4.0, ((1, 32),), jnp.float32)
    target_points = bell_draw(splits[1], (3, TARGETS), 1.0, 4.0, ((1, 16),), jnp.float32)
    source_potential = draw_source_potential(jax.random.fold_in(splits[5], 71), 0)
    target_potential = draw_target_potential(jax.random.fold_in(splits[5], 71), 0)
    neighbours = draw_neighbours(jax.random.fold_in(splits[5], 71), 0)
    return {"source_points": source_points, "target_points": target_points, "source_potential": source_potential, "target_potential": target_potential, "neighbours": neighbours}


EPS = 0.02


def block_terms(packed, target_grid, target_level):
    source_block, source_level, listed_ids, listed = packed
    target_pick = target_grid[:, listed_ids]
    level_pick = target_level[listed_ids]
    first = source_block[0][:, None, None] - target_pick[0][None]
    second = source_block[1][:, None, None] - target_pick[1][None]
    third = source_block[2][:, None, None] - target_pick[2][None]
    pair_cost = 0.5 * (first * first + second * second + third * third)
    row_score = (level_pick[None] - pair_cost) / EPS
    row_score = jnp.where(listed[None, :, None], row_score, -jnp.inf)
    row_top = jnp.max(row_score, axis=(1, 2))
    row_mass = jnp.sum(jnp.exp(row_score - row_top[:, None, None]), axis=(1, 2))
    row_update = -EPS * (row_top + jnp.log(row_mass))
    col_score = (source_level[:, None, None] - pair_cost) / EPS
    col_top = jnp.max(col_score, axis=0)
    col_mass = jnp.sum(jnp.exp(col_score - col_top[None]), axis=0)
    col_top = jnp.where(listed[:, None], col_top, -jnp.inf)
    col_mass = jnp.where(listed[:, None], col_mass, jnp.zeros_like(col_mass))
    return row_update, col_top, col_mass


def reference(source_points, target_points, source_potential, target_potential, neighbours):
    source_grid = source_points.reshape(3, ROW_BLOCKS, BLOCK).transpose(1, 0, 2)
    target_grid = target_points.reshape(3, COL_BLOCKS, BLOCK)
    listed = neighbours >= 0
    listed_ids = jnp.where(listed, neighbours, 0).astype(jnp.int32)
    segment_ids = jnp.where(listed, neighbours, COL_BLOCKS).astype(jnp.int32).reshape(-1)
    source_dual = source_potential
    target_dual = target_potential
    for sweep in range(ITERS):
        source_level = source_dual.reshape(ROW_BLOCKS, BLOCK)
        target_level = target_dual.reshape(COL_BLOCKS, BLOCK)

        def per_block(packed):
            return block_terms(packed, target_grid, target_level)

        row_update, col_top, col_mass = lax.map(per_block, (source_grid, source_level, listed_ids, listed))
        col_top = col_top.reshape(-1, BLOCK)
        col_mass = col_mass.reshape(-1, BLOCK)
        column_peak = jax.ops.segment_max(col_top, segment_ids, num_segments=COL_BLOCKS + 1)
        column_peak = column_peak.at[COL_BLOCKS].set(jnp.zeros((BLOCK,), column_peak.dtype))
        shifted = col_mass * jnp.exp(col_top - column_peak[segment_ids])
        column_mass = jax.ops.segment_sum(shifted, segment_ids, num_segments=COL_BLOCKS + 1)
        col_update = -EPS * (column_peak[:COL_BLOCKS] + jnp.log(column_mass[:COL_BLOCKS]))
        source_dual = 0.5 * (source_dual + row_update.reshape(-1))
        target_dual = 0.5 * (target_dual + col_update.reshape(-1))
    return source_dual, target_dual
```

```python
import functools
import math

import jax
import jax.numpy as jnp
from jax import lax
from jax.experimental import pallas as pl
from jax.experimental.pallas import tpu as pltpu
from jax.sharding import PartitionSpec as P

BLOCK = 256
ITERS = 2
EPS = 0.02
SCALE = math.log2(math.e) / EPS
BACK = -EPS * math.log(2.0)
NEG = -1e30
LANES = 128
F32 = jnp.float32


def split(values):
    first = values.astype(jnp.bfloat16).astype(F32)
    rest = values - first
    second = rest.astype(jnp.bfloat16).astype(F32)
    third = (rest - second).astype(jnp.bfloat16).astype(F32)
    return first, second, third


def factors(values, streamed):
    first, second, third = split(values)
    if streamed:
        rows = (first, second, first, second, third, first)
    else:
        rows = (first, first, second, second, first, third)
    none = jnp.zeros_like(first)
    return jnp.concatenate((*rows, none, none), axis=0).astype(jnp.bfloat16)


def half_norm(points):
    return 0.5 * (points[0:1] * points[0:1] + points[1:2] * points[1:2] + points[2:3] * points[2:3])


def with_level(points, level):
    return jnp.concatenate((SCALE * points, SCALE * (level - half_norm(points))), axis=0)


def with_one(points):
    return jnp.concatenate((points, jnp.ones_like(points[0:1])), axis=0)


def span(lists, row, lo, size):
    width = lists.shape[1]

    def before(bound):
        at = jnp.int32(0)
        steps = [width >> s for s in range(1, width.bit_length())] + [1]
        for step in steps:
            value = lists[row, at + (step - 1)]
            at = at + jnp.where((value >= 0) & (value < bound), step, 0)
        return at

    start = before(lo)
    return start, before(lo + size) - start


def tops(block):
    return jnp.max(block.reshape(-1, 8, block.shape[-1]), axis=0)


def sums(block):
    return jnp.sum(block.reshape(-1, 8, block.shape[-1]), axis=0)


def joined(top, mass):
    peak = jnp.max(top, axis=0, keepdims=True)
    total = jnp.sum(mass * jnp.exp2(top - peak), axis=0, keepdims=True)
    return jnp.where(total > 0, peak + jnp.log2(total), NEG)


def pair_loop(lists, lo, row, size, product, absorb, carry, bufs, peaks):
    start, count = span(lists, row, lo, size)
    last = jnp.maximum(count - 1, 0)

    def column(turn):
        value = lists[row, jnp.minimum(start + jnp.minimum(turn, last), lists.shape[1] - 1)]
        return jnp.clip(value - lo, 0, size - 1)

    def fill(turn, slot):
        block = product(column(turn))
        bufs[slot][...] = block
        peaks[slot][...] = tops(block)

    @pl.when(count > 0)
    def _():
        fill(0, 0)

    def two(half, carry):
        turn = 2 * half
        carry = absorb(column(turn), True, bufs[0], peaks[0], carry)
        fill(turn + 1, 1)
        carry = absorb(column(turn + 1), turn + 1 < count, bufs[1], peaks[1], carry)
        fill(turn + 2, 0)
        return carry

    return lax.fori_loop(0, (count + 1) // 2, two, carry)


def row_kernel(copies, lo_ref, lists, source, target, level, out, left, right, buf0, buf1, peak0, peak1, result):
    block = BLOCK
    rows = source.shape[1] // block
    size = target.shape[1] // block
    lo = lo_ref[0] * size
    for b in range(rows):
        right[b] = factors(with_one(source[:, b * block : (b + 1) * block]), False)

    def build(k, _):
        at = pl.ds(pl.multiple_of(k * block, block), block)
        left[k] = factors(with_level(target[:, at], level[:, at]), True)
        return 0

    lax.fori_loop(0, size, build, 0, unroll=4)

    def one_row(b, _):
        def product(k):
            return lax.dot_general(
                left[k], right[b], (((0,), (0,)), ((), ())), preferred_element_type=F32
            )

        def absorb(k, valid, buf, peak, carry):
            top, mass = carry
            new = jnp.maximum(top, peak[...])
            part = sums(jnp.exp2(buf[...].reshape(-1, 8, block) - new[None]).reshape(block, block))
            if valid is not True:
                part = jnp.where(valid, part, 0.0)
            return new, mass * jnp.exp2(top - new) + part

        zero = (jnp.full((8, block), NEG, F32), jnp.zeros((8, block), F32))
        top, mass = pair_loop(
            lists, lo, b, size, product, absorb, zero, (buf0, buf1), (peak0, peak1)
        )
        result[b] = joined(top, mass)
        return 0

    lax.fori_loop(0, rows, one_row, 0)
    wide = block // LANES
    for b in range(rows):
        line = result[b] - SCALE * half_norm(source[:, b * block : (b + 1) * block])
        for part in range(wide):
            piece = line[:, part * LANES : (part + 1) * LANES]
            out[:, b * wide + part : b * wide + part + 1, :] = jnp.broadcast_to(
                piece[None], (copies, 1, LANES)
            )


def row_level(pieces, old):
    peak = jnp.max(pieces, axis=0)
    total = jnp.sum(jnp.exp2(pieces - peak[None]), axis=0)
    return 0.5 * (old + BACK * (peak + jnp.log2(total)))


def column_kernel(
    fresh, lo_ref, lists, source, target, level, *rest
):
    if fresh:
        out, left, right, buf0, buf1, peak0, peak1, top_ref, mass_ref = rest
        now = level[...]
    else:
        pieces, out, left, right, buf0, buf1, peak0, peak1, top_ref, mass_ref = rest
        now = row_level(pieces[...], level[...])
    block = BLOCK
    wide = block // LANES
    rows = source.shape[1] // block
    size = target.shape[1] // block
    lo = lo_ref[0] * size
    for b in range(rows):
        line = jnp.concatenate(
            [now[b * wide + part : b * wide + part + 1] for part in range(wide)], axis=1
        )
        here = factors(with_level(source[:, b * block : (b + 1) * block], line), True)
        left[b] = here.astype(F32).T.astype(jnp.bfloat16)

    def build(k, _):
        at = pl.ds(pl.multiple_of(k * block, block), block)
        right[k] = factors(with_one(target[:, at]), False)
        top_ref[k] = jnp.full((8, block), NEG, F32)
        mass_ref[k] = jnp.zeros((8, block), F32)
        return 0

    lax.fori_loop(0, size, build, 0, unroll=4)

    def one_row(b, _):
        def product(k):
            return jnp.dot(left[b], right[k], preferred_element_type=F32)

        def absorb(k, valid, buf, peak, carry):
            top = top_ref[k]
            new = jnp.maximum(top, peak[...])
            part = sums(jnp.exp2(buf[...].reshape(-1, 8, block) - new[None]).reshape(block, block))
            if valid is not True:
                part = jnp.where(valid, part, 0.0)
            mass_ref[k] = mass_ref[k] * jnp.exp2(top - new) + part
            top_ref[k] = new
            return carry

        pair_loop(lists, lo, b, size, product, absorb, 0, (buf0, buf1), (peak0, peak1))
        return 0

    lax.fori_loop(0, rows, one_row, 0)
    each = size // out.shape[0]

    def finish(k, _):
        at = pl.ds(pl.multiple_of(k * block, block), block)
        line = joined(top_ref[k], mass_ref[k]) - SCALE * half_norm(target[:, at])
        for part in range(wide):
            out[k // each, pl.ds((k % each) * wide + part, 1), :] = line[
                :, part * LANES : (part + 1) * LANES
            ]
        return 0

    lax.fori_loop(0, size, finish, 0, unroll=4)


def combine_kernel(place_ref, pieces, level, out):
    lines = pieces.shape[1]
    old = level[place_ref[0]]
    new = row_level(pieces[...], old)
    out[...] = jnp.broadcast_to(new[None], out.shape)


def last_kernel(pieces, level, out):
    out[...] = row_level(pieces[...], level[...])


SMEM = pl.BlockSpec(memory_space=pltpu.SMEM)
VMEM = pl.BlockSpec(memory_space=pltpu.VMEM)


def call(body, out, ins, scratch=(), name=None):
    return pl.pallas_call(
        body,
        out_shape=jax.ShapeDtypeStruct(out, F32),
        in_specs=ins,
        out_specs=VMEM,
        scratch_shapes=list(scratch),
        name=name,
    )


def buffers():
    return [pltpu.VMEM((BLOCK, BLOCK), F32)] * 2 + [pltpu.VMEM((8, BLOCK), F32)] * 2


def exchanged(array, axis):
    return lax.all_to_all(array, axis, 0, 0, tiled=True)


def on_device(source_points, target_points, source_potential, target_potential, neighbours):
    n_row = lax.axis_size("row")
    n_col = lax.axis_size("col")
    rows = source_points.shape[1] // BLOCK
    size = target_points.shape[1] // BLOCK
    col = lax.axis_index("col").astype(jnp.int32).reshape(1)
    row = lax.axis_index("row").astype(jnp.int32).reshape(1)
    source_lines = source_points.shape[1] // LANES
    target_lines = target_points.shape[1] // LANES
    share = target_lines // n_row
    source_level = source_potential.reshape(source_lines, LANES)
    target_level = target_potential.reshape(n_row, share, LANES)

    def row_phase(level, name):
        return call(
            functools.partial(row_kernel, n_col),
            (n_col, source_lines, LANES),
            [SMEM, SMEM, VMEM, VMEM, VMEM],
            [
                pltpu.VMEM((size, 32, BLOCK), jnp.bfloat16),
                pltpu.VMEM((rows, 32, BLOCK), jnp.bfloat16),
                *buffers(),
                pltpu.VMEM((rows, 1, BLOCK), F32),
            ],
            name,
        )(col, neighbours, source_points, target_points, level.reshape(1, -1))

    def column_phase(level, pieces, name):
        more = [] if pieces is None else [pieces]
        return call(
            functools.partial(column_kernel, pieces is None),
            (n_row, share, LANES),
            [SMEM, SMEM, VMEM, VMEM, VMEM] + [VMEM] * len(more),
            [
                pltpu.VMEM((rows, BLOCK, 32), jnp.bfloat16),
                pltpu.VMEM((size, 32, BLOCK), jnp.bfloat16),
                *buffers(),
                pltpu.VMEM((size, 8, BLOCK), F32),
                pltpu.VMEM((size, 8, BLOCK), F32),
            ],
            name,
        )(col, neighbours, source_points, target_points, level, *more)

    def column_level(pieces, level, name):
        spread = call(combine_kernel, pieces.shape, [SMEM, VMEM, VMEM], (), name)(row, pieces, level)
        return exchanged(spread, "row")

    def last_level(pieces, level, name):
        return call(last_kernel, level.shape, [VMEM, VMEM], (), name)(pieces, level)

    row_parts = exchanged(row_phase(target_level, "rows_0"), "col")
    column_parts = exchanged(column_phase(source_level, None, "columns_0"), "row")
    target_1 = column_level(column_parts, target_level, "combine_0")
    column_parts_1 = exchanged(column_phase(source_level, row_parts, "columns_1"), "row")
    row_parts_1 = exchanged(row_phase(target_1, "rows_1"), "col")
    source_1 = last_level(row_parts, source_level, "last_0")
    target_2 = column_level(column_parts_1, target_1, "combine_1")
    source_2 = last_level(row_parts_1, source_1, "last_1")
    return source_2.reshape(-1), target_2.reshape(-1)


def solution(mesh):
    in_specs = (P(None, "row"), P(None, "col"), P("row"), P("col"), P("row", None))
    return jax.shard_map(
        on_device, mesh=mesh, in_specs=in_specs, out_specs=(P("row"), P("col")), check_vma=False
    )
```

```python
import functools
import math

import jax
import jax.numpy as jnp
from jax import lax
from jax.experimental import pallas as pl
from jax.experimental.pallas import tpu as pltpu
from jax.sharding import PartitionSpec as P

BLOCK = 256
ITERS = 2
EPS = 0.02
SCALE = math.log2(math.e) / EPS
BACK = -EPS * math.log(2.0)
NEG = -1e30
LANES = 128
F32 = jnp.float32


def split(values):
    first = values.astype(jnp.bfloat16).astype(F32)
    rest = values - first
    second = rest.astype(jnp.bfloat16).astype(F32)
    third = (rest - second).astype(jnp.bfloat16).astype(F32)
    return first, second, third


def factors(values, streamed):
    first, second, third = split(values)
    if streamed:
        rows = (first, second, first, second, third, first)
    else:
        rows = (first, first, second, second, first, third)
    none = jnp.zeros_like(first)
    return jnp.concatenate((*rows, none, none), axis=0).astype(jnp.bfloat16)


def half_norm(points):
    return 0.5 * (points[0:1] * points[0:1] + points[1:2] * points[1:2] + points[2:3] * points[2:3])


def with_level(points, level):
    return jnp.concatenate((SCALE * points, SCALE * (level - half_norm(points))), axis=0)


def with_one(points):
    return jnp.concatenate((points, jnp.ones_like(points[0:1])), axis=0)


def span(lists, row, lo, size):
    width = lists.shape[1]

    def before(bound):
        at = jnp.int32(0)
        steps = [width >> s for s in range(1, width.bit_length())] + [1]
        for step in steps:
            value = lists[row, at + (step - 1)]
            at = at + jnp.where((value >= 0) & (value < bound), step, 0)
        return at

    start = before(lo)
    return start, before(lo + size) - start


def tops(block):
    return jnp.max(block.reshape(-1, 8, block.shape[-1]), axis=0)


def joined(top, mass):
    peak = jnp.max(top, axis=0, keepdims=True)
    total = jnp.sum(mass * jnp.exp2(top - peak), axis=0, keepdims=True)
    return jnp.where(total > 0, peak + jnp.log2(total), NEG)


def listed(lists, codes, lo, size):
    spans = [span(lists, row, lo, size) for row in range(lists.shape[0])]
    codes[0] = 0
    total = jnp.int32(0)
    for row, (start, count) in enumerate(spans):

        def put(turn, _, row=row, start=start, total=total):
            value = lists[row, start + turn] - lo
            codes[total + turn] = row * size + jnp.clip(value, 0, size - 1)
            return 0

        lax.fori_loop(0, count, put, 0)
        total = total + count
    codes[codes.shape[0] - 1] = total


def pair_loop(codes, size, chunk, product, place, tops_ref, mass_ref, bufs, peaks):
    count = codes[codes.shape[0] - 1]
    last = jnp.maximum(count - 1, 0)
    shift = size.bit_length() - 1
    each = len(bufs) // 2

    def pair(turn):
        code = codes[jnp.minimum(turn, last)]
        return code >> shift, code & (size - 1)

    def fill(turn, slot):
        row, column = pair(turn)
        peak = None
        for at in range(0, BLOCK, chunk):
            part = product(row, column, at, chunk)
            bufs[slot][at : at + chunk] = part
            here = tops(part)
            peak = here if peak is None else jnp.maximum(peak, here)
        peaks[slot][...] = peak

    def absorb(turn, slot, sure):
        k = place(*pair(turn))
        top = tops_ref[k]
        new = jnp.maximum(top, peaks[slot][...])
        mass = None
        for at in range(0, BLOCK, chunk):
            part = bufs[slot][at : at + chunk].reshape(-1, 8, BLOCK)
            here = jnp.sum(jnp.exp2(part - new[None]), axis=0)
            mass = here if mass is None else mass + here
        if not sure:
            mass = jnp.where(turn < count, mass, 0.0)
        mass_ref[k] = mass_ref[k] * jnp.exp2(top - new) + mass
        tops_ref[k] = new

    for slot in range(each):
        fill(slot, slot)

    def turns(step, _):
        turn = 2 * each * step
        for slot in range(each):
            fill(turn + each + slot, each + slot)
            absorb(turn + slot, slot, slot == 0)
        for slot in range(each):
            fill(turn + 2 * each + slot, slot)
            absorb(turn + each + slot, each + slot, False)
        return 0

    lax.fori_loop(0, (count + 2 * each - 1) // (2 * each), turns, 0)


def cleared(tops_ref, mass_ref, k):
    tops_ref[k] = jnp.full(tops_ref.shape[1:], NEG, F32)
    mass_ref[k] = jnp.zeros(mass_ref.shape[1:], F32)


def row_kernel(codes, source, target, level, out, left, right, tops_ref, mass_ref, *work):
    block = BLOCK
    wide = block // LANES
    rows = source.shape[1] // block
    size = target.shape[1] // block
    for b in range(rows):
        right[b] = factors(with_one(source[:, b * block : (b + 1) * block]), False)
        cleared(tops_ref, mass_ref, b)

    def build(k, _):
        at = pl.ds(pl.multiple_of(k * block, block), block)
        left[k] = factors(with_level(target[:, at], level[:, at]), True)
        return 0

    lax.fori_loop(0, size, build, 0, unroll=4)

    def product(row, column, at, chunk):
        return lax.dot_general(
            left[column][:, at : at + chunk],
            right[row],
            (((0,), (0,)), ((), ())),
            preferred_element_type=F32,
        )

    half = len(work) // 2
    pair_loop(
        codes, size, 128, product, lambda row, column: row, tops_ref, mass_ref, work[:half], work[half:]
    )
    for b in range(rows):
        line = joined(tops_ref[b], mass_ref[b]) - SCALE * half_norm(
            source[:, b * block : (b + 1) * block]
        )
        for part in range(wide):
            piece = line[:, part * LANES : (part + 1) * LANES]
            out[:, b * wide + part : b * wide + part + 1, :] = jnp.broadcast_to(
                piece[None], (out.shape[0], 1, LANES)
            )


def new_level(pieces, old):
    peak = jnp.max(pieces, axis=0)
    total = jnp.sum(jnp.exp2(pieces - peak[None]), axis=0)
    return 0.5 * (old + BACK * (peak + jnp.log2(total)))


def column_kernel(fresh, source, target, level, *rest):
    if fresh:
        column, lists, out, codes, left, right, tops_ref, mass_ref, *work = rest
        now = level[...]
        listed(lists, codes, column[0] * right.shape[0], right.shape[0])
    else:
        codes, pieces, out, level_out, left, right, tops_ref, mass_ref, *work = rest
        now = new_level(pieces[...], level[...])
        level_out[...] = now
    block = BLOCK
    wide = block // LANES
    rows = source.shape[1] // block
    size = target.shape[1] // block
    for b in range(rows):
        line = jnp.concatenate(
            [now[b * wide + part : b * wide + part + 1] for part in range(wide)], axis=1
        )
        here = factors(with_level(source[:, b * block : (b + 1) * block], line), True)
        left[b] = here.astype(F32).T.astype(jnp.bfloat16)

    def build(k, _):
        at = pl.ds(pl.multiple_of(k * block, block), block)
        right[k] = factors(with_one(target[:, at]), False)
        cleared(tops_ref, mass_ref, k)
        return 0

    lax.fori_loop(0, size, build, 0, unroll=4)

    def product(row, column, at, chunk):
        return jnp.dot(left[row][at : at + chunk], right[column], preferred_element_type=F32)

    half = len(work) // 2
    pair_loop(
        codes, size, 64, product, lambda row, column: column, tops_ref, mass_ref, work[:half], work[half:]
    )
    each = size // out.shape[0]

    def finish(piece, _):
        for e in range(each):
            k = piece * each + e
            at = pl.ds(pl.multiple_of(k * block, block), block)
            line = joined(tops_ref[k], mass_ref[k]) - SCALE * half_norm(target[:, at])
            for part in range(wide):
                out[piece, e * wide + part : e * wide + part + 1, :] = line[
                    :, part * LANES : (part + 1) * LANES
                ]
        return 0

    lax.fori_loop(0, out.shape[0], finish, 0, unroll=4)


def combine_kernel(place_ref, pieces, level, out):
    out[...] = jnp.broadcast_to(new_level(pieces[...], level[place_ref[0]])[None], out.shape)


def last_kernel(pieces, level, out):
    out[...] = new_level(pieces[...], level[...])


SMEM = pl.BlockSpec(memory_space=pltpu.SMEM)
VMEM = pl.BlockSpec(memory_space=pltpu.VMEM)


def call(body, outs, ins, scratch=(), name=None):
    several = isinstance(outs, list)
    shapes = outs if several else [outs]
    shaped = [s if isinstance(s, jax.ShapeDtypeStruct) else jax.ShapeDtypeStruct(s, F32) for s in shapes]
    specs = [SMEM if s.dtype == jnp.int32 else VMEM for s in shaped]
    return pl.pallas_call(
        body,
        out_shape=shaped if several else shaped[0],
        in_specs=ins,
        out_specs=specs if several else specs[0],
        scratch_shapes=list(scratch),
        compiler_params=pltpu.CompilerParams(vmem_limit_bytes=24 << 20),
        name=name,
    )


def scratch(left, right, places):
    return [
        pltpu.VMEM(left, jnp.bfloat16),
        pltpu.VMEM(right, jnp.bfloat16),
        *[pltpu.VMEM((places, 8, BLOCK), F32)] * 2,
        *[pltpu.VMEM((BLOCK, BLOCK), F32)] * 4,
        *[pltpu.VMEM((8, BLOCK), F32)] * 4,
    ]


def exchanged(array, axis):
    return lax.all_to_all(array, axis, 0, 0, tiled=True)


def on_device(source_points, target_points, source_potential, target_potential, neighbours):
    n_row = lax.axis_size("row")
    n_col = lax.axis_size("col")
    rows = source_points.shape[1] // BLOCK
    size = target_points.shape[1] // BLOCK
    col = lax.axis_index("col").astype(jnp.int32).reshape(1)
    row = lax.axis_index("row").astype(jnp.int32).reshape(1)
    source_lines = source_points.shape[1] // LANES
    share = target_points.shape[1] // LANES // n_row
    source_level = source_potential.reshape(source_lines, LANES)
    target_level = target_potential.reshape(n_row, share, LANES)
    codes_shape = jax.ShapeDtypeStruct((neighbours.size + LANES,), jnp.int32)
    column_scratch = scratch((rows, BLOCK, 32), (size, 32, BLOCK), size)
    row_scratch = scratch((size, 32, BLOCK), (rows, 32, BLOCK), rows)
    column_out = (n_row, share, LANES)
    row_out = (n_col, source_lines, LANES)

    def row_phase(codes, level, name):
        return call(row_kernel, row_out, [SMEM, VMEM, VMEM, VMEM], row_scratch, name)(
            codes, source_points, target_points, level.reshape(1, -1)
        )

    def column_level(pieces, level, name):
        spread = call(combine_kernel, pieces.shape, [SMEM, VMEM, VMEM], (), name)(row, pieces, level)
        return exchanged(spread, "row")

    columns_0, codes = call(
        functools.partial(column_kernel, True),
        [column_out, codes_shape],
        [VMEM, VMEM, VMEM, SMEM, SMEM],
        column_scratch,
        "columns_0",
    )(source_points, target_points, source_level, col, neighbours)
    column_pieces_0 = exchanged(columns_0, "row")
    row_pieces_0 = exchanged(row_phase(codes, target_level, "rows_0"), "col")
    target_1 = column_level(column_pieces_0, target_level, "combine_0")
    columns_1, source_1 = call(
        functools.partial(column_kernel, False),
        [column_out, source_level.shape],
        [VMEM, VMEM, VMEM, SMEM, VMEM],
        column_scratch,
        "columns_1",
    )(source_points, target_points, source_level, codes, row_pieces_0)
    column_pieces_1 = exchanged(columns_1, "row")
    rows_1 = row_phase(codes, target_1, "rows_1")
    column_pieces_1, rows_1 = lax.optimization_barrier((column_pieces_1, rows_1))
    target_2 = column_level(column_pieces_1, target_1, "combine_1")
    row_pieces_1 = exchanged(rows_1, "col")
    source_2 = call(last_kernel, source_level.shape, [VMEM, VMEM], (), "last")(row_pieces_1, source_1)
    return source_2.reshape(-1), target_2.reshape(-1)


def solution(mesh):
    in_specs = (P(None, "row"), P(None, "col"), P("row"), P("col"), P("row", None))
    return jax.shard_map(
        on_device, mesh=mesh, in_specs=in_specs, out_specs=(P("row"), P("col")), check_vma=False
    )
```

```python
import functools
import math

import jax
import jax.numpy as jnp
from jax import lax
from jax.experimental import pallas as pl
from jax.experimental.pallas import tpu as pltpu
from jax.sharding import PartitionSpec as P


BLOCK = 256
EPS = 0.02
SCALE = math.log2(math.e) / EPS
BACK = -EPS * math.log(2.0)
NEG = -1e30
LANES = 128
TURN = 4
F32 = jnp.float32


def split(values):
    first = values.astype(jnp.bfloat16).astype(F32)
    rest = values - first
    second = rest.astype(jnp.bfloat16).astype(F32)
    third = (rest - second).astype(jnp.bfloat16).astype(F32)
    return first, second, third


def factors(values, streamed):
    first, second, third = split(values)
    if streamed:
        rows = (first, second, first, second, third, first)
    else:
        rows = (first, first, second, second, first, third)
    none = jnp.zeros_like(first)
    return jnp.concatenate((*rows, none, none), axis=0).astype(jnp.bfloat16)


def half_norm(points):
    return 0.5 * (points[0:1] * points[0:1] + points[1:2] * points[1:2] + points[2:3] * points[2:3])


def with_level(points, level):
    return jnp.concatenate((SCALE * points, SCALE * (level - half_norm(points))), axis=0)


def with_one(points):
    return jnp.concatenate((points, jnp.ones_like(points[0:1])), axis=0)


def span(lists, row, lo, size):
    width = lists.shape[1]

    def before(bound):
        at = jnp.int32(0)
        steps = [width >> s for s in range(1, width.bit_length())] + [1]
        for step in steps:
            value = lists[row, at + (step - 1)]
            at = at + jnp.where((value >= 0) & (value < bound), step, 0)
        return at

    start = before(lo)
    return start, before(lo + size) - start


def tops(block):
    return jnp.max(block.reshape(-1, 8, block.shape[-1]), axis=0)


def joined(top, mass):
    peak = jnp.max(top, axis=0, keepdims=True)
    total = jnp.sum(mass * jnp.exp2(top - peak), axis=0, keepdims=True)
    return jnp.where(total > 0, peak + jnp.log2(total), NEG)


def listed(lists, codes, lo, size):
    spans = [span(lists, row, lo, size) for row in range(lists.shape[0])]
    codes[0] = 0
    total = jnp.int32(0)
    for row, (start, count) in enumerate(spans):

        def put(turn, _, row=row, start=start, total=total):
            value = lists[row, start + turn] - lo
            codes[total + turn] = row * size + jnp.clip(value, 0, size - 1)
            return 0

        lax.fori_loop(0, count, put, 0)
        total = total + count
    codes[codes.shape[0] - 1] = total


def pair_loop(codes, size, chunk, product, place, tops_ref, mass_ref, bufs, peaks):
    count = codes[codes.shape[0] - 1]
    last = jnp.maximum(count - 1, 0)
    shift = size.bit_length() - 1
    each = len(bufs) // 2

    def pair(turn):
        code = codes[jnp.minimum(turn, last)]
        return code >> shift, code & (size - 1)

    def fill(turn, slot):
        row, column = pair(turn)
        peak = None
        for at in range(0, BLOCK, chunk):
            part = product(row, column, at, chunk)
            bufs[slot][at : at + chunk] = part
            here = tops(part)
            peak = here if peak is None else jnp.maximum(peak, here)
        peaks[slot][...] = peak

    def absorb(turn, slot, sure):
        k = place(*pair(turn))
        top = tops_ref[k]
        new = jnp.maximum(top, peaks[slot][...])
        mass = None
        for at in range(0, BLOCK, chunk):
            part = bufs[slot][at : at + chunk].reshape(-1, 8, BLOCK)
            here = jnp.sum(jnp.exp2(part - new[None]), axis=0)
            mass = here if mass is None else mass + here
        if not sure:
            mass = jnp.where(turn < count, mass, 0.0)
        mass_ref[k] = mass_ref[k] * jnp.exp2(top - new) + mass
        tops_ref[k] = new

    for slot in range(each):
        fill(slot, slot)

    def turns(step, _):
        turn = 2 * each * step
        for slot in range(each):
            fill(turn + each + slot, each + slot)
            absorb(turn + slot, slot, slot == 0)
        for slot in range(each):
            fill(turn + 2 * each + slot, slot)
            absorb(turn + each + slot, each + slot, False)
        return 0

    lax.fori_loop(0, (count + 2 * each - 1) // (2 * each), turns, 0)


def cleared(tops_ref, mass_ref, k):
    tops_ref[k] = jnp.full(tops_ref.shape[1:], NEG, F32)
    mass_ref[k] = jnp.zeros(mass_ref.shape[1:], F32)


def row_kernel(codes, source, target, level, out, left, right, tops_ref, mass_ref, *work):
    block = BLOCK
    wide = block // LANES
    rows = source.shape[1] // block
    size = target.shape[1] // block
    for b in range(rows):
        right[b] = factors(with_one(source[:, b * block : (b + 1) * block]), False)
        cleared(tops_ref, mass_ref, b)

    def build(k, _):
        at = pl.ds(pl.multiple_of(k * block, block), block)
        left[k] = factors(with_level(target[:, at], level[:, at]), True)
        return 0

    lax.fori_loop(0, size, build, 0, unroll=4)

    def product(row, column, at, chunk):
        return lax.dot_general(
            left[column][:, at : at + chunk],
            right[row],
            (((0,), (0,)), ((), ())),
            preferred_element_type=F32,
        )

    half = len(work) // 2
    pair_loop(
        codes, size, 128, product, lambda row, column: row, tops_ref, mass_ref, work[:half], work[half:]
    )
    for b in range(rows):
        line = joined(tops_ref[b], mass_ref[b]) - SCALE * half_norm(
            source[:, b * block : (b + 1) * block]
        )
        for part in range(wide):
            piece = line[:, part * LANES : (part + 1) * LANES]
            out[:, b * wide + part : b * wide + part + 1, :] = jnp.broadcast_to(
                piece[None], (out.shape[0], 1, LANES)
            )


def new_level(pieces, old):
    peak = jnp.max(pieces, axis=0)
    total = jnp.sum(jnp.exp2(pieces - peak[None]), axis=0)
    return 0.5 * (old + BACK * (peak + jnp.log2(total)))


def column_kernel(fresh, source, target, level, *rest):
    if fresh:
        column, lists, out, codes, left, right, tops_ref, mass_ref, *work = rest
        now = level[...]
        listed(lists, codes, column[0] * right.shape[0], right.shape[0])
    else:
        codes, pieces, out, level_out, left, right, tops_ref, mass_ref, *work = rest
        now = new_level(pieces[...], level[...])
        level_out[...] = now
    block = BLOCK
    wide = block // LANES
    rows = source.shape[1] // block
    size = target.shape[1] // block
    for b in range(rows):
        line = jnp.concatenate(
            [now[b * wide + part : b * wide + part + 1] for part in range(wide)], axis=1
        )
        here = factors(with_level(source[:, b * block : (b + 1) * block], line), True)
        left[b] = here.astype(F32).T.astype(jnp.bfloat16)

    def build(k, _):
        at = pl.ds(pl.multiple_of(k * block, block), block)
        right[k] = factors(with_one(target[:, at]), False)
        cleared(tops_ref, mass_ref, k)
        return 0

    lax.fori_loop(0, size, build, 0, unroll=4)

    def product(row, column, at, chunk):
        return jnp.dot(left[row][at : at + chunk], right[column], preferred_element_type=F32)

    half = len(work) // 2
    pair_loop(
        codes, size, 64, product, lambda row, column: column, tops_ref, mass_ref, work[:half], work[half:]
    )
    each = size // out.shape[0]

    def finish(piece, _):
        for e in range(each):
            k = piece * each + e
            at = pl.ds(pl.multiple_of(k * block, block), block)
            line = joined(tops_ref[k], mass_ref[k]) - SCALE * half_norm(target[:, at])
            for part in range(wide):
                out[piece, e * wide + part : e * wide + part + 1, :] = line[
                    :, part * LANES : (part + 1) * LANES
                ]
        return 0

    lax.fori_loop(0, out.shape[0], finish, 0, unroll=4)


def combine_kernel(place_ref, pieces, level, out):
    out[...] = jnp.broadcast_to(new_level(pieces[...], level[place_ref[0]])[None], out.shape)


def last_kernel(pieces, level, out):
    out[...] = new_level(pieces[...], level[...])


SMEM = pl.BlockSpec(memory_space=pltpu.SMEM)
VMEM = pl.BlockSpec(memory_space=pltpu.VMEM)


def call(body, outs, ins, scratch=(), limit=24 << 20):
    several = isinstance(outs, list)
    shapes = outs if several else [outs]
    shaped = [s if isinstance(s, jax.ShapeDtypeStruct) else jax.ShapeDtypeStruct(s, F32) for s in shapes]
    specs = [SMEM if s.dtype == jnp.int32 else VMEM for s in shaped]
    return pl.pallas_call(
        body,
        out_shape=shaped if several else shaped[0],
        in_specs=ins,
        out_specs=specs if several else specs[0],
        scratch_shapes=list(scratch),
        compiler_params=pltpu.CompilerParams(vmem_limit_bytes=limit),
    )


def scratch(left, right, places):
    return [
        pltpu.VMEM(left, jnp.bfloat16),
        pltpu.VMEM(right, jnp.bfloat16),
        *[pltpu.VMEM((places, 8, BLOCK), F32)] * 2,
        *[pltpu.VMEM((BLOCK, BLOCK), F32)] * (2 * TURN),
        *[pltpu.VMEM((8, BLOCK), F32)] * (2 * TURN),
    ]


def exchanged(array, axis):
    return lax.all_to_all(array, axis, 0, 0, tiled=True)


def on_device(source_points, target_points, source_potential, target_potential, neighbours):
    n_row = lax.axis_size("row")
    n_col = lax.axis_size("col")
    rows = source_points.shape[1] // BLOCK
    size = target_points.shape[1] // BLOCK
    col = lax.axis_index("col").astype(jnp.int32).reshape(1)
    row = lax.axis_index("row").astype(jnp.int32).reshape(1)
    source_lines = source_points.shape[1] // LANES
    share = target_points.shape[1] // LANES // n_row
    source_level = source_potential.reshape(source_lines, LANES)
    target_level = target_potential.reshape(n_row, share, LANES)
    codes_shape = jax.ShapeDtypeStruct((neighbours.size + LANES,), jnp.int32)
    column_scratch = scratch((rows, BLOCK, 32), (size, 32, BLOCK), size)
    row_scratch = scratch((size, 32, BLOCK), (rows, 32, BLOCK), rows)
    column_out = (n_row, share, LANES)
    row_out = (n_col, source_lines, LANES)

    def row_phase(codes, level):
        return call(row_kernel, row_out, [SMEM, VMEM, VMEM, VMEM], row_scratch)(
            codes, source_points, target_points, level.reshape(1, -1)
        )

    def column_level(pieces, level):
        spread = call(combine_kernel, pieces.shape, [SMEM, VMEM, VMEM], ())(row, pieces, level)
        return exchanged(spread, "row")

    columns_0, codes = call(
        functools.partial(column_kernel, True),
        [column_out, codes_shape],
        [VMEM, VMEM, VMEM, SMEM, SMEM],
        column_scratch,
        60 << 20,
    )(source_points, target_points, source_level, col, neighbours)
    column_pieces_0 = exchanged(columns_0, "row")
    row_pieces_0 = exchanged(row_phase(codes, target_level), "col")
    target_1 = column_level(column_pieces_0, target_level)
    columns_1, source_1 = call(
        functools.partial(column_kernel, False),
        [column_out, source_level.shape],
        [VMEM, VMEM, VMEM, SMEM, VMEM],
        column_scratch,
    )(source_points, target_points, source_level, codes, row_pieces_0)
    column_pieces_1 = exchanged(columns_1, "row")
    rows_1 = row_phase(codes, target_1)
    column_pieces_1, rows_1 = lax.optimization_barrier((column_pieces_1, rows_1))
    row_pieces_1 = exchanged(rows_1, "col")
    spread = call(combine_kernel, column_out, [SMEM, VMEM, VMEM], ())(row, column_pieces_1, target_1)
    target_2 = exchanged(spread, "row")
    source_2 = call(last_kernel, source_level.shape, [VMEM, VMEM], ())(
        row_pieces_1, source_1
    )
    return source_2.reshape(-1), target_2.reshape(-1)


def solution(mesh):
    in_specs = (P(None, "row"), P(None, "col"), P("row"), P("col"), P("row", None))
    return jax.shard_map(
        on_device, mesh=mesh, in_specs=in_specs, out_specs=(P("row"), P("col")), check_vma=False
    )
```

```python
import functools
import math

import jax
import jax.numpy as jnp
from jax import lax
from jax.experimental import pallas as pl
from jax.experimental.pallas import tpu as pltpu
from jax.sharding import Mesh
from jax.sharding import PartitionSpec as P


BLOCK = 256
EPS = 0.02
SCALE = math.log2(math.e) / EPS
BACK = -EPS * math.log(2.0)
NEG = -1e30
LANES = 128
TURN = 4
F32 = jnp.float32


def split(values):
    first = values.astype(jnp.bfloat16).astype(F32)
    rest = values - first
    second = rest.astype(jnp.bfloat16).astype(F32)
    third = (rest - second).astype(jnp.bfloat16).astype(F32)
    return first, second, third


def factors(values, streamed):
    first, second, third = split(values)
    if streamed:
        rows = (first, second, first, second, third, first)
    else:
        rows = (first, first, second, second, first, third)
    none = jnp.zeros_like(first)
    return jnp.concatenate((*rows, none, none), axis=0).astype(jnp.bfloat16)


def half_norm(points):
    return 0.5 * (points[0:1] * points[0:1] + points[1:2] * points[1:2] + points[2:3] * points[2:3])


def with_level(points, level):
    return jnp.concatenate((SCALE * points, SCALE * (level - half_norm(points))), axis=0)


def with_one(points):
    return jnp.concatenate((points, jnp.ones_like(points[0:1])), axis=0)


def span(lists, row, lo, size):
    width = lists.shape[1]

    def before(bound):
        at = jnp.int32(0)
        steps = [width >> s for s in range(1, width.bit_length())] + [1]
        for step in steps:
            value = lists[row, at + (step - 1)]
            at = at + jnp.where((value >= 0) & (value < bound), step, 0)
        return at

    start = before(lo)
    return start, before(lo + size) - start


def tops(block):
    return jnp.max(block.reshape(-1, 8, block.shape[-1]), axis=0)


def joined(top, mass):
    peak = jnp.max(top, axis=0, keepdims=True)
    total = jnp.sum(mass * jnp.exp2(top - peak), axis=0, keepdims=True)
    return jnp.where(total > 0, peak + jnp.log2(total), NEG)


def list_kernel(place, lists, codes):
    size = place[2]
    core = place[1]
    lo = place[0] * 2 * size
    spans = [span(lists, row, lo, 2 * size) for row in range(lists.shape[0])]
    codes[0] = 0
    total = jnp.int32(0)
    for row, (start, count) in enumerate(spans):

        def put(turn, _, row=row, start=start, total=total):
            value = jnp.clip(lists[row, start + turn] - lo, 0, 2 * size - 1)
            codes[total + turn] = row * 2 * size + (value ^ (core * size))
            return 0

        lax.fori_loop(0, count, put, 0)
        total = total + count
    half = (total + 1) // 2
    mine = jnp.clip(total - core * half, 0, half)
    codes[codes.shape[0] - 1] = mine
    codes[codes.shape[0] - 2] = jnp.where(mine > 0, core * half, 0)


def pair_loop(codes, size, chunk, product, place, tops_ref, mass_ref, bufs, peaks):
    count = codes[codes.shape[0] - 1]
    first = codes[codes.shape[0] - 2]
    last = jnp.maximum(count - 1, 0)
    shift = size.bit_length() - 1
    each = len(bufs) // 2

    def pair(turn):
        code = codes[first + jnp.minimum(turn, last)]
        return code >> shift, code & (size - 1)

    def fill(turn, slot):
        row, column = pair(turn)
        peak = None
        for at in range(0, BLOCK, chunk):
            part = product(row, column, at, chunk)
            bufs[slot][at : at + chunk] = part
            here = tops(part)
            peak = here if peak is None else jnp.maximum(peak, here)
        peaks[slot][...] = peak

    def absorb(turn, slot, sure):
        k = place(*pair(turn))
        top = tops_ref[k]
        new = jnp.maximum(top, peaks[slot][...])
        mass = None
        for at in range(0, BLOCK, chunk):
            part = bufs[slot][at : at + chunk].reshape(-1, 8, BLOCK)
            here = jnp.sum(jnp.exp2(part - new[None]), axis=0)
            mass = here if mass is None else mass + here
        if not sure:
            mass = jnp.where(turn < count, mass, 0.0)
        mass_ref[k] = mass_ref[k] * jnp.exp2(top - new) + mass
        tops_ref[k] = new

    for slot in range(each):
        fill(slot, slot)

    def turns(step, _):
        turn = 2 * each * step
        for slot in range(each):
            fill(turn + each + slot, each + slot)
            absorb(turn + slot, slot, slot == 0)
        for slot in range(each):
            fill(turn + 2 * each + slot, slot)
            absorb(turn + each + slot, each + slot, False)
        return 0

    lax.fori_loop(0, (count + 2 * each - 1) // (2 * each), turns, 0)


def cleared(tops_ref, mass_ref, k):
    tops_ref[k] = jnp.full(tops_ref.shape[1:], NEG, F32)
    mass_ref[k] = jnp.zeros(mass_ref.shape[1:], F32)


def wide_line(lines, first):
    return jnp.concatenate(
        [lines[first + part : first + part + 1] for part in range(BLOCK // LANES)], axis=1
    )


def row_kernel(later, place, codes, source, mine, other, *rest):
    if later:
        level, out, left, right, tops_ref, mass_ref, *work = rest
    else:
        level_mine, level_other, out, left, right, tops_ref, mass_ref, *work = rest
    block = BLOCK
    wide = block // LANES
    rows = source.shape[1] // block
    size = mine.shape[1] // block
    for b in range(rows):
        right[b] = factors(with_one(source[:, b * block : (b + 1) * block]), False)
        cleared(tops_ref, mass_ref, b)
    pieces = (level if later else level_mine).shape[0]
    each = size // pieces
    core = place[1]
    for side, points in enumerate((mine, other)):

        def build(piece, _, side=side, points=points):
            if later:
                lines = level[piece, core ^ side]
            else:
                lines = (level_mine, level_other)[side][piece]
            for e in range(each):
                k = piece * each + e
                at = pl.ds(pl.multiple_of(k * block, block), block)
                left[side * size + k] = factors(
                    with_level(points[:, at], wide_line(lines, e * wide)), True
                )
            return 0

        lax.fori_loop(0, pieces, build, 0, unroll=2)
    size = 2 * size

    def product(row, column, at, chunk):
        return lax.dot_general(
            left[column][:, at : at + chunk],
            right[row],
            (((0,), (0,)), ((), ())),
            preferred_element_type=F32,
        )

    half = len(work) // 2
    pair_loop(
        codes, size, 128, product, lambda row, column: row, tops_ref, mass_ref, work[:half], work[half:]
    )
    for b in range(rows):
        line = joined(tops_ref[b], mass_ref[b]) - SCALE * half_norm(
            source[:, b * block : (b + 1) * block]
        )
        for part in range(wide):
            piece = line[:, part * LANES : (part + 1) * LANES]
            out[:, b * wide + part : b * wide + part + 1, :] = jnp.broadcast_to(
                piece[None], (out.shape[0], 1, LANES)
            )


def new_level(pieces, old):
    peak = jnp.max(pieces, axis=0)
    total = jnp.sum(jnp.exp2(pieces - peak[None]), axis=0)
    return 0.5 * (old + BACK * (peak + jnp.log2(total)))


def column_kernel(fresh, place, codes, source, mine, other, level, *rest):
    if fresh:
        out, left, right, tops_ref, mass_ref, *work = rest
        now = level[...]
    else:
        pieces, out, level_out, left, right, tops_ref, mass_ref, *work = rest
        now = new_level(pieces[...], level[...])
        level_out[...] = now
    block = BLOCK
    wide = block // LANES
    rows = source.shape[1] // block
    size = mine.shape[1] // block
    core = place[1]
    for b in range(rows):
        line = wide_line(now, b * wide)
        here = factors(with_level(source[:, b * block : (b + 1) * block], line), True)
        left[b] = here.astype(F32).T.astype(jnp.bfloat16)
    for side, points in enumerate((mine, other)):

        def build(k, _, side=side, points=points):
            at = pl.ds(pl.multiple_of(k * block, block), block)
            right[side * size + k] = factors(with_one(points[:, at]), False)
            cleared(tops_ref, mass_ref, side * size + k)
            return 0

        lax.fori_loop(0, size, build, 0, unroll=4)

    def product(row, column, at, chunk):
        return jnp.dot(left[row][at : at + chunk], right[column], preferred_element_type=F32)

    half = len(work) // 2
    pair_loop(
        codes, 2 * size, 64, product, lambda row, column: column, tops_ref, mass_ref, work[:half], work[half:]
    )
    pieces = out.shape[0] // 2
    each = size // pieces
    for side, points in enumerate((mine, other)):

        def finish(piece, _, side=side, points=points):
            for e in range(each):
                k = piece * each + e
                at = pl.ds(pl.multiple_of(k * block, block), block)
                line = joined(tops_ref[side * size + k], mass_ref[side * size + k])
                line = line - SCALE * half_norm(points[:, at])
                for part in range(wide):
                    out[2 * piece + (core ^ side), e * wide + part : e * wide + part + 1, :] = line[
                        :, part * LANES : (part + 1) * LANES
                    ]
            return 0

        lax.fori_loop(0, pieces, finish, 0, unroll=4)


def combine_kernel(place, pieces, level, out, *own):
    new = new_level(pieces[...], level[place[3]] if own else level[...])
    out[...] = jnp.broadcast_to(new[None], out.shape)
    for ref in own:
        ref[...] = new


def last_kernel(pieces, level, out):
    out[...] = new_level(pieces[...], level[...])


SMEM = pl.BlockSpec(memory_space=pltpu.SMEM)
VMEM = pl.BlockSpec(memory_space=pltpu.VMEM)


def call(body, outs, ins, scratch=(), limit=24 << 20):
    several = isinstance(outs, list)
    shapes = outs if several else [outs]
    shaped = [s if isinstance(s, jax.ShapeDtypeStruct) else jax.ShapeDtypeStruct(s, F32) for s in shapes]
    specs = [SMEM if s.dtype == jnp.int32 else VMEM for s in shaped]
    return pl.pallas_call(
        body,
        out_shape=shaped if several else shaped[0],
        in_specs=ins,
        out_specs=specs if several else specs[0],
        scratch_shapes=list(scratch),
        compiler_params=pltpu.CompilerParams(vmem_limit_bytes=limit),
    )


def scratch(left, right, places):
    return [
        pltpu.VMEM(left, jnp.bfloat16),
        pltpu.VMEM(right, jnp.bfloat16),
        *[pltpu.VMEM((places, 8, BLOCK), F32)] * 2,
        *[pltpu.VMEM((BLOCK, BLOCK), F32)] * (2 * TURN),
        *[pltpu.VMEM((8, BLOCK), F32)] * (2 * TURN),
    ]


def exchanged(array, axis):
    return lax.all_to_all(array, axis, 0, 0, tiled=True)


def on_device(source_points, target_points, source_potential, target_potential, neighbours):
    n_row = lax.axis_size("row")
    n_col = lax.axis_size("y") * lax.axis_size("core")
    rows = source_points.shape[1] // BLOCK
    size = target_points.shape[1] // BLOCK
    core = lax.axis_index("core")
    place = jnp.stack([lax.axis_index("y"), core, size, lax.axis_index("row")]).astype(jnp.int32)
    source_lines = source_points.shape[1] // LANES
    share = target_points.shape[1] // LANES // n_row
    source_level = source_potential.reshape(source_lines, LANES)
    target_level = target_potential.reshape(n_row, share, LANES)
    codes_shape = jax.ShapeDtypeStruct((neighbours.size + LANES,), jnp.int32)
    column_scratch = scratch((rows, BLOCK, 32), (2 * size, 32, BLOCK), 2 * size)
    row_scratch = scratch((2 * size, 32, BLOCK), (rows, 32, BLOCK), rows)
    column_out = (2 * n_row, share, LANES)
    row_out = (n_col, source_lines, LANES)
    both = ("row", "core")
    across = ("y", "core")
    swap = [(0, 1), (1, 0)]

    other_points = lax.ppermute(target_points, "core", swap)
    other_level = lax.ppermute(target_potential, "core", swap)
    other_points, other_level = lax.optimization_barrier((other_points, other_level))
    other_level = other_level.reshape(target_level.shape)
    codes = call(list_kernel, codes_shape, [SMEM, SMEM], ())(place, neighbours)
    points = (source_points, target_points, other_points)

    def row_phase(levels):
        later = len(levels) == 1
        return call(
            functools.partial(row_kernel, later), row_out, [SMEM, SMEM] + [VMEM] * (3 + len(levels)), row_scratch
        )(place, codes, *points, *levels)

    columns_0 = call(
        functools.partial(column_kernel, True), column_out, [SMEM, SMEM] + [VMEM] * 4, column_scratch
    )(place, codes, *points, source_level)
    column_pieces_0 = exchanged(columns_0, both)
    row_pieces_0 = exchanged(row_phase((target_level, other_level)), across)
    spread_0, mine_1 = call(
        combine_kernel, [column_out, target_level.shape[1:]], [SMEM, VMEM, VMEM], ()
    )(place, column_pieces_0, target_level)
    target_1 = exchanged(spread_0, both).reshape(n_row, 2, share, LANES)
    columns_1, source_1 = call(
        functools.partial(column_kernel, False),
        [column_out, source_level.shape],
        [SMEM, SMEM] + [VMEM] * 5,
        column_scratch,
    )(place, codes, *points, source_level, row_pieces_0)
    column_pieces_1 = exchanged(columns_1, both)
    rows_1 = row_phase((target_1,))
    column_pieces_1, rows_1 = lax.optimization_barrier((column_pieces_1, rows_1))
    row_pieces_1 = exchanged(rows_1, across)
    spread = call(combine_kernel, target_level.shape, [SMEM, VMEM, VMEM], ())(place, column_pieces_1, mine_1)
    target_2 = exchanged(spread, "row")
    source_2 = call(last_kernel, source_level.shape, [VMEM, VMEM], ())(
        row_pieces_1, source_1
    )
    return source_2.reshape(-1), target_2.reshape(-1)


def solution(mesh):
    finer = Mesh(mesh.devices.reshape(mesh.shape["row"], -1, 2), ("row", "y", "core"))
    across = ("y", "core")
    in_specs = (P(None, "row"), P(None, across), P("row"), P(across), P("row", None))
    return jax.shard_map(
        on_device, mesh=finer, in_specs=in_specs, out_specs=(P("row"), P(across)), check_vma=False
    )
```
